32 devices in a mesh: groups: 2 (over y), section: 2 (over core), row: 2 (over x), col: 4 (over z).
Axes of the slice: x: 2, y: 2, z: 4, core: 2. Of those that a mesh axis runs over, the one named last changes fastest.
Arguments:
- mid: bfloat16 [2, 768, 8192], P('section', ('groups', 'col'), 'row'), parts along dimension 1, may hold values from -12000 to 12000
- query_grad: bfloat16 [2, 768, 8192], P('section', ('groups', 'row'), 'col'), parts along dimension 1, may hold values from -6 to 6
- top_grad: bfloat16 [768, 8192], P(('groups', 'col'), 'row'), parts along dimension 0, may hold values from -6 to 6
- w_query: bfloat16 [2, 8192, 8192], P('section', 'row', 'col'), may hold values from -0.0625 to 0.0625
- gain: float32 [2, 8192], P('section', 'row'), may hold values from 0.5 to 1.5
Outputs:
- weight_grad: bfloat16 [4, 8192, 8192], P(('groups', 'section'), 'row', 'col'), parts along dimension 0
- residual_grad: bfloat16 [2, 768, 8192], P('section', ('groups', 'col'), 'row'), parts along dimension 1
The draws below stay inside these ranges and needn't reach their ends.
There are 2 independent parts, one for each index of `groups`. The reference program is written for one: setup_inputs(seed, part) draws one part's arguments, and reference() takes and returns one part's arrays. A program takes and returns all parts, laid end to end along the dimension named above; an argument that names none is the same for every part. Nothing has to cross between parts.
All inputs are finite; a program needn't handle non-finite values.
Results may differ from the reference program's by a relative error of at most 0.0085.
Values may be sent and summed in bfloat16 or wider, within the bound.
A program may use at most 128 MiB of HBM per device.

```python
import math
import jax
import jax.numpy as jnp
from jax import lax

D = 8192
HQ = 8192
TOK = 384
SECTIONS = 2
N_COL = 4


def draw_mid(key, part):
    key_base, key_rows, key_cols, key_tail = jax.random.split(key, 4)
    rise = jnp.exp(math.log(3.0) * jnp.arange(D, dtype=jnp.float32) / (D - 1))
    base = jax.random.truncated_normal(key_base, -4.0, 4.0, (SECTIONS, TOK, D), jnp.float32)
    uniform_tail = jax.random.uniform(key_tail, (SECTIONS, TOK, D), jnp.float32, 0.0001, 1.0)
    heavy = jnp.exp(-0.7 * jnp.log(uniform_tail)) / 10.0
    rows = jnp.exp(jax.random.uniform(key_rows, (SECTIONS, TOK, 1), jnp.float32, math.log(0.5), math.log(5.0)))
    cols = jnp.exp(jax.random.uniform(key_cols, (SECTIONS, 1, D), jnp.float32, math.log(0.4), math.log(4.0)))
    return (base * heavy * rows * cols * rise / math.sqrt(3.0)).astype(jnp.bfloat16)


def with_spikes(drawn, stream_key, source, target, blocks, factor):
    def block_of(axis_at):
        return (jnp.arange(drawn.shape[axis_at]) // (drawn.shape[axis_at] // blocks)).reshape((-1,) + (1,) * (drawn.ndim - 1 - axis_at))

    first = jax.random.permutation(stream_key, blocks)[block_of(target)]
    other_side = (block_of(target) + blocks // 2) % blocks
    return jnp.where((block_of(source) == first) | (block_of(source) == other_side), factor * drawn, drawn)


def shard_levels(rng, extent, pieces, smallest, high):
    level, own = 1.0, jax.random.fold_in(rng, 6)
    for position, blocks in pieces:
        draws = jnp.exp(jax.random.uniform(jax.random.fold_in(own, position), (blocks,), jnp.float32, smallest / len(pieces), high / len(pieces)))
        level = level * jnp.repeat(draws, extent[position] // blocks).reshape([-1 if axis == position else 1 for axis in range(len(extent))])
    return level


def gaussian(stream_key, extent, width, bound, shards=(), held_as=jnp.bfloat16):
    drawn = width * jax.random.normal(stream_key, extent, jnp.float32)
    if shards:
        drawn = drawn * shard_levels(stream_key, extent, shards, -0.22, 0.18)
    return jnp.clip(drawn, -bound, bound).astype(held_as)


def bell_draw_with(own_key, shape, scale, limit, cuts, heavy, kind=jnp.bfloat16):
    drawn = scale * jax.random.normal(own_key, shape, jnp.float32)
    if cuts:
        drawn = drawn * shard_levels(own_key, shape, cuts, -0.22, 0.18)
    return jnp.clip(with_spikes(drawn, jax.random.fold_in(own_key, 3), *heavy), -limit, limit).astype(kind)


def setup_inputs(seed: int = 0, part: int = 0) -> dict:
    key_of = jax.random.split(jax.random.key(seed), 6)
    part_keys = jax.random.split(jax.random.fold_in(key_of[5], part), 6)
    return {
        "mid": draw_mid(jax.random.fold_in(jax.random.fold_in(key_of[5], part), 71), part),
        "query_grad": bell_draw_with(part_keys[1], (SECTIONS, TOK, HQ), 1.0, 6.0, ((0, 2), (1, 2), (2, 4)), (2, 1, 4, 2.0)),
        "top_grad": gaussian(part_keys[2], (TOK, D), 1.0, 6.0, ((0, 4), (1, 2))),
        "w_query": gaussian(key_of[3], (SECTIONS, D, HQ), D ** -0.5, 0.0625, ((0, 2), (1, 2), (2, 4))),
        "gain": jnp.clip(1.0 + 0.1 * jax.random.normal(key_of[4], (SECTIONS, D), jnp.float32), 0.5, 1.5),
    }


EPSILON = 1e-05

def reference(mid, query_grad, top_grad, w_query, gain):
    block = HQ // N_COL
    terms = []
    grads = []
    for layer in range(SECTIONS):
        x_float = mid[layer].astype(jnp.float32)
        gains = gain[layer]
        inverse = lax.rsqrt(lax.optimization_barrier(jnp.sum(x_float * x_float, axis=1)) / D + EPSILON)
        normed = (x_float * inverse[:, None] * gains).astype(jnp.bfloat16)
        normed_grad = jnp.zeros((TOK, D), jnp.float32)
        for index in range(N_COL):
            part_grad = query_grad[layer][:, index * block:(index + 1) * block]
            part_weight = w_query[layer][:, index * block:(index + 1) * block]
            partial_sum = jnp.dot(part_grad, part_weight.T, preferred_element_type=jnp.float32).astype(jnp.bfloat16)
            partial_sum = lax.optimization_barrier(partial_sum)
            normed_grad = normed_grad + partial_sum.astype(jnp.float32)
        product = lax.optimization_barrier(jnp.sum(x_float * gains * normed_grad, axis=1))
        term = inverse[:, None] * gains * normed_grad - x_float * (inverse ** 3 * product / D)[:, None]
        terms.append(term)
        contracted = jnp.dot(normed.T, query_grad[layer], preferred_element_type=jnp.float32)
        grads.append((contracted * TOK ** (-0.5)).astype(jnp.bfloat16))
    total = top_grad.astype(jnp.float32)
    outputs = [None] * SECTIONS
    for layer in range(SECTIONS - 1, -1, -1):
        total = total + terms[layer]
        outputs[layer] = total.astype(jnp.bfloat16)
    return (jnp.stack(grads), jnp.stack(outputs))
```

```python
import functools

import jax
import jax.numpy as jnp
from jax import lax
from jax.experimental import pallas as pl
from jax.experimental.pallas import tpu as pltpu
from jax.sharding import PartitionSpec as P

EPSILON = 1e-05
LANES = 128
ROWS = 16
F32 = jnp.float32
BF16 = jnp.bfloat16


def lane_sums(value):
    total = value[:, :LANES]
    for at in range(LANES, value.shape[1], LANES):
        total = total + value[:, at : at + LANES]
    return total


def push(src, dst, send, recv, axis, peer):
    return pltpu.make_async_remote_copy(
        src_ref=src,
        dst_ref=dst,
        send_sem=send,
        recv_sem=recv,
        device_id={axis: peer},
        device_id_type=pl.DeviceIdType.MESH,
    )


def kernel(
    n_sec, n_row, n_col, chunks, halves, parts,
    mid, query, top, gain, w_hbm,
    res, normed_hbm, query_hbm,
    w_v, mid_all, query_all, part, from_left, from_right,
    squares, squares_in, prods, prods_in, grad, term, later, total, normed, scales,
    w_sem, x_right, x_left, x_recv, ag_right, ag_left, ag_recv,
    rs_right, rs_left, rs_from_left, rs_from_right,
    sq_send, sq_recv, pr_send, pr_recv, term_send, term_recv, out_sem,
):
    me_s, me_r, me_c = (lax.axis_index(a) for a in ("section", "row", "col"))
    tokens, width = mid.shape
    subs = query.shape[0]
    fc = width // chunks
    tile = min(512, fc)
    full = width * n_row
    has_left, has_right = me_c > 0, me_c < n_col - 1

    def w_copy(ch):
        rows = pl.ds(pl.multiple_of(ch * fc, fc), fc)
        return pltpu.make_async_copy(w_hbm.at[rows], w_v.at[rows], w_sem.at[ch])

    for ch in range(chunks):
        w_copy(ch).start()

    barrier = pltpu.get_barrier_semaphore()

    def greet(axis, peer):
        pl.semaphore_signal(
            barrier, inc=1, device_id={axis: peer}, device_id_type=pl.DeviceIdType.MESH
        )

    for k in range(1, n_row):
        greet("row", lax.rem(me_r + k, n_row))
    for k in range(1, n_sec):
        greet("section", lax.rem(me_s + k, n_sec))
    pl.when(has_left)(lambda: greet("col", me_c - 1))
    pl.when(has_right)(lambda: greet("col", me_c + 1))
    beside = (me_c + n_col - 1) // n_col + (2 * n_col - 2 - me_c) // n_col
    pl.semaphore_wait(barrier, n_row - 1 + n_sec - 1 + beside)

    def x_send(k, sub, right):
        piece = me_r - k if right else me_r + k
        shard = piece * subs + sub
        src = query.at[sub] if k == 0 else query_all.at[shard]
        return push(
            src, query_all.at[shard], (x_right if right else x_left).at[shard], x_recv.at[shard],
            "row", me_r + 1 if right else me_r - 1,
        )

    def x_sends(k, right):
        if right:
            return (me_r - k >= 0) & (me_r < n_row - 1)
        return (me_r + k < n_row) & (me_r > 0)

    def order(right):
        return range(subs) if right else range(subs - 1, -1, -1)

    for right in (True, False):
        @pl.when(x_sends(0, right))
        def _():
            for sub in order(right):
                x_send(0, sub, right).start()

    half = tokens // halves

    def ag_send(k, h, right):
        shard = me_c - k if right else me_c + k
        rows = pl.ds(h * half, half)
        src = mid.at[rows] if k == 0 else mid_all.at[shard, rows]
        return push(
            src, mid_all.at[shard, rows], (ag_right if right else ag_left).at[shard, h],
            ag_recv.at[shard, h], "col", me_c + 1 if right else me_c - 1,
        )

    def ag_sends(k, right):
        if right:
            return (me_c - k >= 0) & has_right
        return (me_c + k < n_col) & has_left

    for h in range(halves):
        for right in (True, False):
            pl.when(ag_sends(0, right))(lambda: ag_send(0, h, right).start())

    def ag_step(k):
        for h in range(halves):
            for right in (True, False):
                shard = me_c - k if right else me_c + k

                @pl.when((shard >= 0) if right else (shard < n_col))
                def _():
                    rows = pl.ds(h * half, half)
                    got = mid_all.at[shard, rows]
                    pltpu.make_async_copy(got, got, ag_recv.at[shard, h]).wait()
                    if k < n_col - 1:
                        pl.when(ag_sends(k, right))(lambda: ag_send(k, h, right).start())

    def product(shard, count, load, first):
        def lap(ch, _):
            if first:
                w_copy(ch).wait()
            for t in range(fc // tile):
                rows = pl.ds(pl.multiple_of(ch * fc + t * tile, tile), tile)
                value = lax.dot_general(
                    load(), w_v[rows, :], (((1,), (1,)), ((), ())), preferred_element_type=F32
                ).astype(BF16)
                for at in range(count):
                    part[shard + at, ch, :, t * tile : (t + 1) * tile] = value[
                        at * tokens : (at + 1) * tokens
                    ]
            return 0

        lax.fori_loop(0, chunks, lap, 0)

    mid_all[me_c] = mid[...]
    for sub in range(subs):
        query_all[me_r * subs + sub] = query[sub]
    product(me_r * subs, subs, lambda: query[...].reshape(subs * tokens, query.shape[2]), True)

    @pl.when(jnp.logical_not(has_left))
    def _():
        from_left[0] = jnp.zeros(from_left.shape[1:], BF16)

    @pl.when(jnp.logical_not(has_right))
    def _():
        from_right[n_col - 1] = jnp.zeros(from_right.shape[1:], BF16)

    def x_step(k, at):
        for right in (True, False):
            piece = me_r - k if right else me_r + k
            sub = at if right else subs - 1 - at
            shard = piece * subs + sub

            @pl.when((piece >= 0) if right else (piece < n_row))
            def _():
                got = query_all.at[shard]
                pltpu.make_async_copy(got, got, x_recv.at[shard]).wait()
                if k < n_row - 1:
                    pl.when(x_sends(k, right))(lambda: x_send(k, sub, right).start())
                product(shard, 1, lambda: query_all[shard], False)

    def rs_send(shard, ch, right):
        return push(
            part.at[shard, ch], (from_left if right else from_right).at[shard, ch],
            (rs_right if right else rs_left).at[shard, ch],
            (rs_from_left if right else rs_from_right).at[shard, ch],
            "col", me_c + 1 if right else me_c - 1,
        )

    def rs_shard(step, right):
        if right:
            shard = n_col - 1 - (step - me_c)
            return shard, (step >= me_c) & (shard > me_c)
        shard = step - (n_col - 1 - me_c)
        return shard, (shard >= 0) & (shard < me_c)

    def rs_wait(shard, ch, right):
        got = (from_left if right else from_right).at[shard, ch]
        pltpu.make_async_copy(
            got, got, (rs_from_left if right else rs_from_right).at[shard, ch]
        ).wait()

    def rs_step(step):
        for ch in range(chunks):
            for right in (True, False):
                shard, valid = rs_shard(step, right)

                @pl.when(valid)
                def _():
                    @pl.when(has_left if right else has_right)
                    def _():
                        rs_wait(shard, ch, right)
                        came = from_left if right else from_right

                        def lap(i, _):
                            rows = pl.ds(pl.multiple_of(i * ROWS, ROWS), ROWS)
                            part[shard, ch, rows, :] = (
                                part[shard, ch, rows, :].astype(F32)
                                + came[shard, ch, rows, :].astype(F32)
                            ).astype(BF16)
                            return 0

                        lax.fori_loop(0, tokens // ROWS, lap, 0)

                    rs_send(shard, ch, right).start()

    steps = [(k, at) for k in range(1, n_row) for at in range(subs)]
    for k, at in steps[:-1]:
        x_step(k, at)
    if subs > 1:
        rs_step(0)
    if n_col > 1:
        ag_step(1)
    for k, at in steps[-1:]:
        x_step(k, at)
    if subs == 1:
        rs_step(0)
    query_out = pltpu.make_async_copy(query_all, query_hbm, out_sem.at[0])
    query_out.start()
    for step in range(1, n_col - 1):
        ag_step(step + 1)
        if step == n_col - 2:
            break
        rs_step(step)

    def square_lap(i, _):
        shard, at = i // (tokens // ROWS), i % (tokens // ROWS)
        rows = pl.ds(pl.multiple_of(at * ROWS, ROWS), ROWS)
        value = mid_all[shard, rows, :].astype(F32)
        squares[shard, rows, :] = lane_sums(value * value)
        return 0

    lax.fori_loop(0, n_col * (tokens // ROWS), square_lap, 0)

    def sq_copy(k):
        return push(
            squares, squares_in.at[me_r], sq_send.at[k], sq_recv.at[me_r],
            "row", lax.rem(me_r + k, n_row),
        )

    def pr_copy(k):
        return push(
            prods, prods_in.at[me_r], pr_send.at[k], pr_recv.at[me_r],
            "row", lax.rem(me_r + k, n_row),
        )

    def await_from(ref, sem):
        for k in range(1, n_row):
            peer = lax.rem(me_r + k, n_row)
            got = ref.at[peer]
            pltpu.make_async_copy(got, got, sem.at[peer]).wait()

    for k in range(1, n_row):
        sq_copy(k).start()
    if n_col > 2:
        rs_step(n_col - 2)
    await_from(squares_in, sq_recv)

    def normed_lap(i, _):
        shard, at = i // (tokens // ROWS), i % (tokens // ROWS)
        rows = pl.ds(pl.multiple_of(at * ROWS, ROWS), ROWS)
        summed = squares[shard, rows, :]
        for k in range(1, n_row):
            summed = summed + squares_in[lax.rem(me_r + k, n_row), shard, rows, :]
        inverse = lax.rsqrt(jnp.sum(summed, axis=1, keepdims=True) / full + EPSILON)
        scales[shard, rows, :] = jnp.broadcast_to(inverse, (ROWS, LANES))
        value = mid_all[shard, rows, :].astype(F32)
        normed[shard, rows, :] = (value * inverse * gain[...]).astype(BF16)
        return 0

    lax.fori_loop(0, n_col * (tokens // ROWS), normed_lap, 0)
    normed_out = pltpu.make_async_copy(normed, normed_hbm, out_sem.at[1])
    normed_out.start()

    prods[...] = jnp.zeros(prods.shape, F32)
    for ch in range(chunks):
        pl.when(has_left)(lambda: rs_wait(me_c, ch, True))
        pl.when(has_right)(lambda: rs_wait(me_c, ch, False))
        cols = slice(ch * fc, (ch + 1) * fc)

        def grad_lap(i, _):
            rows = pl.ds(pl.multiple_of(i * ROWS, ROWS), ROWS)
            value = (
                part[me_c, ch, rows, :].astype(F32)
                + from_left[me_c, ch, rows, :].astype(F32)
                + from_right[me_c, ch, rows, :].astype(F32)
            ) * gain[:, cols]
            grad[rows, cols] = value
            prods[rows, :] += lane_sums(mid[rows, cols].astype(F32) * value)
            return 0

        lax.fori_loop(0, tokens // ROWS, grad_lap, 0)
    for k in range(1, n_row):
        pr_copy(k).start()
    await_from(prods_in, pr_recv)

    piece = tokens // parts

    def term_copy(to, at):
        rows = pl.ds(at * piece, piece)
        return push(
            term.at[rows], later.at[me_s, rows], term_send.at[to, at], term_recv.at[me_s, at],
            "section", to,
        )

    for at in range(parts):
        def term_lap(i, _):
            rows = pl.ds(pl.multiple_of(at * piece + i * ROWS, ROWS), ROWS)
            summed = prods[rows, :]
            for k in range(1, n_row):
                summed = summed + prods_in[lax.rem(me_r + k, n_row), rows, :]
            inverse = scales[me_c, rows, :][:, :1]
            scale = inverse**3 * jnp.sum(summed, axis=1, keepdims=True) / full
            own = inverse * grad[rows, :] - mid[rows, :].astype(F32) * scale
            term[rows, :] = own.astype(BF16)
            total[rows, :] = top[rows, :].astype(F32) + own
            return 0

        lax.fori_loop(0, piece // ROWS, term_lap, 0)
        for to in range(n_sec - 1):
            pl.when(me_s > to)(lambda: term_copy(to, at).start())
    for at in range(parts):
        for source in range(1, n_sec):
            @pl.when(me_s < source)
            def _():
                span = pl.ds(at * piece, piece)
                got = later.at[source, span]
                pltpu.make_async_copy(got, got, term_recv.at[source, at]).wait()

                def later_lap(i, _):
                    rows = pl.ds(pl.multiple_of(at * piece + i * ROWS, ROWS), ROWS)
                    total[rows, :] += later[source, rows, :].astype(F32)
                    return 0

                lax.fori_loop(0, piece // ROWS, later_lap, 0)

        def res_lap(i, _):
            rows = pl.ds(pl.multiple_of(at * piece + i * ROWS, ROWS), ROWS)
            res[rows, :] = total[rows, :].astype(BF16)
            return 0

        lax.fori_loop(0, piece // ROWS, res_lap, 0)

    for right in (True, False):
        for k in range(n_row - 1):
            @pl.when(x_sends(k, right))
            def _():
                for sub in order(right):
                    x_send(k, sub, right).wait_send()
        for k in range(n_col - 1):
            @pl.when(ag_sends(k, right))
            def _():
                for h in range(halves):
                    ag_send(k, h, right).wait_send()
        for step in range(n_col - 1):
            shard, valid = rs_shard(step, right)

            @pl.when(valid)
            def _():
                for ch in range(chunks):
                    rs_send(shard, ch, right).wait_send()
    for k in range(1, n_row):
        sq_copy(k).wait_send()
        pr_copy(k).wait_send()
    for to in range(n_sec - 1):
        @pl.when(me_s > to)
        def _():
            for at in range(parts):
                term_copy(to, at).wait_send()
    query_out.wait()
    normed_out.wait()


def body(mid, query_grad, top_grad, w_query, gain):
    n_sec, n_row, n_col = (lax.axis_size(a) for a in ("section", "row", "col"))
    tokens, width = mid.shape[1:]
    rows, depth = query_grad.shape[1:]
    subs = rows // tokens
    chunks, halves, parts = 4, 2, 3
    fc = width // chunks
    vmem = pl.BlockSpec(memory_space=pltpu.VMEM)
    hbm = pl.BlockSpec(memory_space=pl.ANY)
    dma = pltpu.SemaphoreType.DMA
    residual, normed, query = pl.pallas_call(
        functools.partial(kernel, n_sec, n_row, n_col, chunks, halves, parts),
        out_shape=(
            jax.ShapeDtypeStruct((tokens, width), BF16),
            jax.ShapeDtypeStruct((n_col, tokens, width), BF16),
            jax.ShapeDtypeStruct((n_col, tokens, depth), BF16),
        ),
        in_specs=[vmem, vmem, vmem, vmem, hbm],
        out_specs=(vmem, hbm, hbm),
        scratch_shapes=[
            pltpu.VMEM((width, depth), BF16),
            pltpu.VMEM((n_col, tokens, width), BF16),
            pltpu.VMEM((n_col, tokens, depth), BF16),
            pltpu.VMEM((n_col, chunks, tokens, fc), BF16),
            pltpu.VMEM((n_col, chunks, tokens, fc), BF16),
            pltpu.VMEM((n_col, chunks, tokens, fc), BF16),
            pltpu.VMEM((n_col, tokens, LANES), F32),
            pltpu.VMEM((n_row, n_col, tokens, LANES), F32),
            pltpu.VMEM((tokens, LANES), F32),
            pltpu.VMEM((n_row, tokens, LANES), F32),
            pltpu.VMEM((tokens, width), F32),
            pltpu.VMEM((tokens, width), BF16),
            pltpu.VMEM((n_sec, tokens, width), BF16),
            pltpu.VMEM((tokens, width), F32),
            pltpu.VMEM((n_col, tokens, width), BF16),
            pltpu.VMEM((n_col, tokens, LANES), F32),
            dma((chunks,)),
            dma((n_col,)), dma((n_col,)), dma((n_col,)),
            dma((n_col, halves)), dma((n_col, halves)), dma((n_col, halves)),
            dma((n_col, chunks)), dma((n_col, chunks)),
            dma((n_col, chunks)), dma((n_col, chunks)),
            dma((n_row,)), dma((n_row,)), dma((n_row,)), dma((n_row,)),
            dma((n_sec, parts)), dma((n_sec, parts)),
            dma((2,)),
        ],
        compiler_params=pltpu.CompilerParams(
            collective_id=0, has_side_effects=True, vmem_limit_bytes=58 * 1024 * 1024
        ),
    )(mid[0], query_grad[0].reshape(subs, tokens, depth), top_grad, gain, w_query[0])
    total_rows = n_col * tokens
    contracted = lax.dot_general(
        normed.reshape(total_rows, width),
        query.reshape(total_rows, depth),
        (((0,), (0,)), ((), ())),
        preferred_element_type=F32,
    )
    weight_grad = (contracted * total_rows ** (-0.5)).astype(BF16)[None]
    return (weight_grad, residual[None])


def solution(mesh):
    return jax.shard_map(
        body,
        mesh=mesh,
        in_specs=(
            P("section", ("groups", "col"), "row"),
            P("section", ("groups", "row"), "col"),
            P(("groups", "col"), "row"),
            P("section", "row", "col"),
            P("section", "row"),
        ),
        out_specs=(P(("groups", "section"), "row", "col"), P("section", ("groups", "col"), "row")),
        check_vma=False,
    )
```

```python
import functools

import jax
import jax.numpy as jnp
from jax import lax
from jax.experimental import pallas as pl
from jax.experimental.pallas import tpu as pltpu
from jax.sharding import PartitionSpec as P

EPSILON = 1e-05
LANES = 128
ROWS = 16
F32 = jnp.float32
BF16 = jnp.bfloat16


def lane_sums(value):
    total = value[:, :LANES]
    for at in range(LANES, value.shape[1], LANES):
        total = total + value[:, at : at + LANES]
    return total


def push(src, dst, send, recv, axis, peer):
    return pltpu.make_async_remote_copy(
        src_ref=src,
        dst_ref=dst,
        send_sem=send,
        recv_sem=recv,
        device_id={axis: peer},
        device_id_type=pl.DeviceIdType.MESH,
    )


def kernel(
    n_sec, n_row, n_col, chunks, halves, parts,
    mid, query, top, gain, w_hbm,
    res, normed_hbm, query_hbm,
    w_v, mid_all, query_all, part, from_left, from_right,
    squares, squares_in, prods, prods_in, grad, term, later, total, normed, turned, scales,
    w_sem, x_right, x_left, x_recv, ag_right, ag_left, ag_recv,
    rs_right, rs_left, rs_from_left, rs_from_right,
    sq_send, sq_recv, pr_send, pr_recv, term_send, term_recv, out_sem,
):
    me_s, me_r, me_c = (lax.axis_index(a) for a in ("section", "row", "col"))
    tokens, width = mid.shape
    subs = query.shape[0]
    fc = width // chunks
    tile = min(1024, fc)
    full = width * n_row
    has_left, has_right = me_c > 0, me_c < n_col - 1

    def w_copy(ch):
        rows = pl.ds(pl.multiple_of(ch * fc, fc), fc)
        return pltpu.make_async_copy(w_hbm.at[rows], w_v.at[rows], w_sem.at[ch])

    for ch in range(chunks):
        w_copy(ch).start()

    barrier = pltpu.get_barrier_semaphore()

    def greet(axis, peer):
        pl.semaphore_signal(
            barrier, inc=1, device_id={axis: peer}, device_id_type=pl.DeviceIdType.MESH
        )

    for k in range(1, n_row):
        greet("row", lax.rem(me_r + k, n_row))
    for k in range(1, n_sec):
        greet("section", lax.rem(me_s + k, n_sec))
    pl.when(has_left)(lambda: greet("col", me_c - 1))
    pl.when(has_right)(lambda: greet("col", me_c + 1))
    beside = (me_c + n_col - 1) // n_col + (2 * n_col - 2 - me_c) // n_col
    pl.semaphore_wait(barrier, n_row - 1 + n_sec - 1 + beside)

    def x_send(k, sub, right):
        piece = me_r - k if right else me_r + k
        shard = piece * subs + sub
        src = query.at[sub] if k == 0 else query_all.at[shard]
        return push(
            src, query_all.at[shard], (x_right if right else x_left).at[shard], x_recv.at[shard],
            "row", me_r + 1 if right else me_r - 1,
        )

    def x_sends(k, right):
        if right:
            return (me_r - k >= 0) & (me_r < n_row - 1)
        return (me_r + k < n_row) & (me_r > 0)

    def order(right):
        return range(subs) if right else range(subs - 1, -1, -1)

    for right in (True, False):
        @pl.when(x_sends(0, right))
        def _():
            for sub in order(right):
                x_send(0, sub, right).start()

    half = tokens // halves

    def ag_send(k, h, right):
        shard = me_c - k if right else me_c + k
        rows = pl.ds(h * half, half)
        src = mid.at[rows] if k == 0 else mid_all.at[shard, rows]
        return push(
            src, mid_all.at[shard, rows], (ag_right if right else ag_left).at[shard, h],
            ag_recv.at[shard, h], "col", me_c + 1 if right else me_c - 1,
        )

    def ag_sends(k, right):
        if right:
            return (me_c - k >= 0) & has_right
        return (me_c + k < n_col) & has_left

    for h in range(halves):
        for right in (True, False):
            pl.when(ag_sends(0, right))(lambda: ag_send(0, h, right).start())

    def ag_step(k):
        for h in range(halves):
            for right in (True, False):
                shard = me_c - k if right else me_c + k

                @pl.when((shard >= 0) if right else (shard < n_col))
                def _():
                    rows = pl.ds(h * half, half)
                    got = mid_all.at[shard, rows]
                    pltpu.make_async_copy(got, got, ag_recv.at[shard, h]).wait()
                    if k < n_col - 1:
                        pl.when(ag_sends(k, right))(lambda: ag_send(k, h, right).start())

    def product(shard, count, load, first):
        def lap(ch, _):
            if first:
                w_copy(ch).wait()
            for t in range(fc // tile):
                rows = pl.ds(pl.multiple_of(ch * fc + t * tile, tile), tile)
                value = lax.dot_general(
                    load(), w_v[rows, :], (((1,), (1,)), ((), ())), preferred_element_type=F32
                ).astype(BF16)
                for at in range(count):
                    part[shard + at, ch, :, t * tile : (t + 1) * tile] = value[
                        at * tokens : (at + 1) * tokens
                    ]
            return 0

        lax.fori_loop(0, chunks, lap, 0)

    mid_all[me_c] = mid[...]
    for sub in range(subs):
        query_all[me_r * subs + sub] = query[sub]
    product(me_r * subs, subs, lambda: query[...].reshape(subs * tokens, query.shape[2]), True)

    @pl.when(jnp.logical_not(has_left))
    def _():
        from_left[0] = jnp.zeros(from_left.shape[1:], BF16)

    @pl.when(jnp.logical_not(has_right))
    def _():
        from_right[n_col - 1] = jnp.zeros(from_right.shape[1:], BF16)

    def sq_copy(k, shard):
        return push(
            squares.at[shard], squares_in.at[me_r, shard], sq_send.at[k, shard],
            sq_recv.at[me_r, shard], "row", lax.rem(me_r + k, n_row),
        )

    def square(shard):
        def lap(i, _):
            rows = pl.ds(pl.multiple_of(i * ROWS, ROWS), ROWS)
            value = mid_all[shard, rows, :].astype(F32)
            squares[shard, rows, :] = lane_sums(value * value)
            return 0

        lax.fori_loop(0, tokens // ROWS, lap, 0)
        for k in range(1, n_row):
            sq_copy(k, shard).start()

    def normalize(shard):
        for k in range(1, n_row):
            peer = lax.rem(me_r + k, n_row)
            got = squares_in.at[peer, shard]
            pltpu.make_async_copy(got, got, sq_recv.at[peer, shard]).wait()

        def lap(i, _):
            rows = pl.ds(pl.multiple_of(i * ROWS, ROWS), ROWS)
            summed = squares[shard, rows, :]
            for k in range(1, n_row):
                summed = summed + squares_in[lax.rem(me_r + k, n_row), shard, rows, :]
            inverse = lax.rsqrt(jnp.sum(summed, axis=1, keepdims=True) / full + EPSILON)
            scales[shard, rows, :] = jnp.broadcast_to(inverse, (ROWS, LANES))
            value = mid_all[shard, rows, :].astype(F32)
            at = pl.ds(pl.multiple_of(shard * tokens + i * ROWS, ROWS), ROWS)
            normed[at, :] = (value * inverse * gain[...]).astype(BF16)
            return 0

        lax.fori_loop(0, tokens // ROWS, lap, 0)

    def normalize_step(k):
        pl.when(me_c - k >= 0)(lambda: normalize(me_c - k))
        pl.when(me_c + k < n_col)(lambda: normalize(me_c + k))

    def square_step(k):
        pl.when(me_c - k >= 0)(lambda: square(me_c - k))
        pl.when(me_c + k < n_col)(lambda: square(me_c + k))

    square(me_c)

    def x_step(k, at):
        for right in (True, False):
            piece = me_r - k if right else me_r + k
            sub = at if right else subs - 1 - at
            shard = piece * subs + sub

            @pl.when((piece >= 0) if right else (piece < n_row))
            def _():
                got = query_all.at[shard]
                pltpu.make_async_copy(got, got, x_recv.at[shard]).wait()
                if k < n_row - 1:
                    pl.when(x_sends(k, right))(lambda: x_send(k, sub, right).start())
                product(shard, 1, lambda: query_all[shard], False)

    def rs_send(shard, ch, right):
        return push(
            part.at[shard, ch], (from_left if right else from_right).at[shard, ch],
            (rs_right if right else rs_left).at[shard, ch],
            (rs_from_left if right else rs_from_right).at[shard, ch],
            "col", me_c + 1 if right else me_c - 1,
        )

    def rs_shard(step, right):
        if right:
            shard = n_col - 1 - (step - me_c)
            return shard, (step >= me_c) & (shard > me_c)
        shard = step - (n_col - 1 - me_c)
        return shard, (shard >= 0) & (shard < me_c)

    def rs_wait(shard, ch, right):
        got = (from_left if right else from_right).at[shard, ch]
        pltpu.make_async_copy(
            got, got, (rs_from_left if right else rs_from_right).at[shard, ch]
        ).wait()

    def rs_first(step):
        for right in (True, False):
            shard, valid = rs_shard(step, right)
            before = shard + 1 if right else shard - 1

            @pl.when(valid & jnp.logical_not(has_left if right else has_right))
            def _():
                for ch in range(chunks):
                    if step:
                        rs_send(before, ch, right).wait_send()
                    rs_send(shard, ch, right).start()

    def rs_step(step):
        for ch in range(chunks):
            for right in (True, False):
                shard, valid = rs_shard(step, right)

                @pl.when(valid & (has_left if right else has_right))
                def _():
                    rs_wait(shard, ch, right)
                    came = from_left if right else from_right

                    def lap(i, _):
                        rows = pl.ds(pl.multiple_of(i * ROWS, ROWS), ROWS)
                        part[shard, ch, rows, :] = (
                            part[shard, ch, rows, :].astype(F32)
                            + came[shard, ch, rows, :].astype(F32)
                        ).astype(BF16)
                        return 0

                    lax.fori_loop(0, tokens // ROWS, lap, 0)
                    rs_send(shard, ch, right).start()

    steps = [(k, at) for k in range(1, n_row) for at in range(subs)]
    for k, at in steps[:-1]:
        x_step(k, at)
    if subs > 1:
        rs_first(0)
    if n_col > 1:
        ag_step(1)
    for k, at in steps[-1:]:
        x_step(k, at)
    if subs == 1:
        rs_first(0)
    query_out = pltpu.make_async_copy(query_all, query_hbm, out_sem.at[0])
    query_out.start()
    if n_col > 1:
        square_step(1)
    normalize(me_c)
    for step in range(1, n_col - 1):
        rs_first(step)
        ag_step(step + 1)
        rs_step(step)
        square_step(step + 1)
        normalize_step(step)
    if n_col > 1:
        normalize_step(n_col - 1)

    def pr_copy(k):
        return push(
            prods, prods_in.at[me_r], pr_send.at[k], pr_recv.at[me_r],
            "row", lax.rem(me_r + k, n_row),
        )

    def await_from(ref, sem):
        for k in range(1, n_row):
            peer = lax.rem(me_r + k, n_row)
            got = ref.at[peer]
            pltpu.make_async_copy(got, got, sem.at[peer]).wait()

    def turn_lap(i, _):
        cols = pl.ds(pl.multiple_of(i * LANES, LANES), LANES)
        turned[cols, :] = normed[:, cols].T
        return 0

    lax.fori_loop(0, width // LANES, turn_lap, 0)
    normed_out = pltpu.make_async_copy(turned, normed_hbm, out_sem.at[1])
    normed_out.start()

    prods[...] = jnp.zeros(prods.shape, F32)
    for ch in range(chunks):
        pl.when(has_left)(lambda: rs_wait(me_c, ch, True))
        pl.when(has_right)(lambda: rs_wait(me_c, ch, False))
        cols = slice(ch * fc, (ch + 1) * fc)

        def grad_lap(i, _):
            rows = pl.ds(pl.multiple_of(i * ROWS, ROWS), ROWS)
            value = (
                part[me_c, ch, rows, :].astype(F32)
                + from_left[me_c, ch, rows, :].astype(F32)
                + from_right[me_c, ch, rows, :].astype(F32)
            ) * gain[:, cols]
            grad[rows, cols] = value
            prods[rows, :] += lane_sums(mid[rows, cols].astype(F32) * value)
            return 0

        lax.fori_loop(0, tokens // ROWS, grad_lap, 0)
    for k in range(1, n_row):
        pr_copy(k).start()
    await_from(prods_in, pr_recv)

    piece = tokens // parts

    def term_copy(to, at):
        rows = pl.ds(at * piece, piece)
        return push(
            term.at[rows], later.at[me_s, rows], term_send.at[to, at], term_recv.at[me_s, at],
            "section", to,
        )

    for at in range(parts):
        def term_lap(i, _):
            rows = pl.ds(pl.multiple_of(at * piece + i * ROWS, ROWS), ROWS)
            summed = prods[rows, :]
            for k in range(1, n_row):
                summed = summed + prods_in[lax.rem(me_r + k, n_row), rows, :]
            inverse = scales[me_c, rows, :][:, :1]
            scale = inverse**3 * jnp.sum(summed, axis=1, keepdims=True) / full
            own = inverse * grad[rows, :] - mid[rows, :].astype(F32) * scale
            term[rows, :] = own.astype(BF16)
            total[rows, :] = top[rows, :].astype(F32) + own
            return 0

        lax.fori_loop(0, piece // ROWS, term_lap, 0)
        for to in range(n_sec - 1):
            pl.when(me_s > to)(lambda: term_copy(to, at).start())
    for at in range(parts):
        for source in range(1, n_sec):
            @pl.when(me_s < source)
            def _():
                span = pl.ds(at * piece, piece)
                got = later.at[source, span]
                pltpu.make_async_copy(got, got, term_recv.at[source, at]).wait()

                def later_lap(i, _):
                    rows = pl.ds(pl.multiple_of(at * piece + i * ROWS, ROWS), ROWS)
                    total[rows, :] += later[source, rows, :].astype(F32)
                    return 0

                lax.fori_loop(0, piece // ROWS, later_lap, 0)

        def res_lap(i, _):
            rows = pl.ds(pl.multiple_of(at * piece + i * ROWS, ROWS), ROWS)
            res[rows, :] = total[rows, :].astype(BF16)
            return 0

        lax.fori_loop(0, piece // ROWS, res_lap, 0)

    for right in (True, False):
        for k in range(n_row - 1):
            @pl.when(x_sends(k, right))
            def _():
                for sub in order(right):
                    x_send(k, sub, right).wait_send()
        for k in range(n_col - 1):
            @pl.when(ag_sends(k, right))
            def _():
                for h in range(halves):
                    ag_send(k, h, right).wait_send()
        for step in range(n_col - 1):
            shard, valid = rs_shard(step, right)

            first = jnp.logical_not(has_left if right else has_right)
            if step < n_col - 2:
                valid = valid & jnp.logical_not(first)

            @pl.when(valid)
            def _():
                for ch in range(chunks):
                    rs_send(shard, ch, right).wait_send()
    for k in range(1, n_row):
        for shard in range(n_col):
            sq_copy(k, shard).wait_send()
        pr_copy(k).wait_send()
    for to in range(n_sec - 1):
        @pl.when(me_s > to)
        def _():
            for at in range(parts):
                term_copy(to, at).wait_send()
    query_out.wait()
    normed_out.wait()


def weight_kernel(scale, left, right, residual, out, residual_out):
    value = jnp.dot(left[...], right[...], preferred_element_type=F32)
    out[...] = (value * scale).astype(BF16)
    residual_out[...] = residual[...]


def body(mid, query_grad, top_grad, w_query, gain):
    n_sec, n_row, n_col = (lax.axis_size(a) for a in ("section", "row", "col"))
    tokens, width = mid.shape[1:]
    rows, depth = query_grad.shape[1:]
    subs = rows // tokens
    chunks, halves, parts = 4, 2, 3
    fc = width // chunks
    vmem = pl.BlockSpec(memory_space=pltpu.VMEM)
    hbm = pl.BlockSpec(memory_space=pl.ANY)
    dma = pltpu.SemaphoreType.DMA
    residual, normed, query = pl.pallas_call(
        functools.partial(kernel, n_sec, n_row, n_col, chunks, halves, parts),
        out_shape=(
            jax.ShapeDtypeStruct((tokens, width), BF16),
            jax.ShapeDtypeStruct((width, n_col * tokens), BF16),
            jax.ShapeDtypeStruct((n_col, tokens, depth), BF16),
        ),
        in_specs=[vmem, vmem, vmem, vmem, hbm],
        out_specs=(vmem, hbm, hbm),
        scratch_shapes=[
            pltpu.VMEM((width, depth), BF16),
            pltpu.VMEM((n_col, tokens, width), BF16),
            pltpu.VMEM((n_col, tokens, depth), BF16),
            pltpu.VMEM((n_col, chunks, tokens, fc), BF16),
            pltpu.VMEM((n_col, chunks, tokens, fc), BF16),
            pltpu.VMEM((n_col, chunks, tokens, fc), BF16),
            pltpu.VMEM((n_col, tokens, LANES), F32),
            pltpu.VMEM((n_row, n_col, tokens, LANES), F32),
            pltpu.VMEM((tokens, LANES), F32),
            pltpu.VMEM((n_row, tokens, LANES), F32),
            pltpu.VMEM((tokens, width), F32),
            pltpu.VMEM((tokens, width), BF16),
            pltpu.VMEM((n_sec, tokens, width), BF16),
            pltpu.VMEM((tokens, width), F32),
            pltpu.VMEM((n_col * tokens, width), BF16),
            pltpu.VMEM((width, n_col * tokens), BF16),
            pltpu.VMEM((n_col, tokens, LANES), F32),
            dma((chunks,)),
            dma((n_col,)), dma((n_col,)), dma((n_col,)),
            dma((n_col, halves)), dma((n_col, halves)), dma((n_col, halves)),
            dma((n_col, chunks)), dma((n_col, chunks)),
            dma((n_col, chunks)), dma((n_col, chunks)),
            dma((n_row, n_col)), dma((n_row, n_col)), dma((n_row,)), dma((n_row,)),
            dma((n_sec, parts)), dma((n_sec, parts)),
            dma((2,)),
        ],
        compiler_params=pltpu.CompilerParams(
            collective_id=0, has_side_effects=True, vmem_limit_bytes=58 * 1024 * 1024
        ),
    )(mid[0], query_grad[0].reshape(subs, tokens, depth), top_grad, gain, w_query[0])
    total_rows = n_col * tokens
    tall = min(512, width)
    weight_grad, residual = pl.pallas_call(
        functools.partial(weight_kernel, total_rows ** (-0.5)),
        grid=(width // tall,),
        out_shape=(
            jax.ShapeDtypeStruct((width, depth), BF16),
            jax.ShapeDtypeStruct((tokens, width), BF16),
        ),
        in_specs=[
            pl.BlockSpec((tall, total_rows), lambda i: (i, 0)),
            pl.BlockSpec((total_rows, depth), lambda i: (0, 0)),
            pl.BlockSpec((tokens, tall), lambda i: (0, i)),
        ],
        out_specs=(
            pl.BlockSpec((tall, depth), lambda i: (i, 0)),
            pl.BlockSpec((tokens, tall), lambda i: (0, i)),
        ),
        compiler_params=pltpu.CompilerParams(vmem_limit_bytes=60 * 1024 * 1024),
    )(normed, query.reshape(total_rows, depth), residual)
    return (weight_grad[None], residual[None])


def solution(mesh):
    return jax.shard_map(
        body,
        mesh=mesh,
        in_specs=(
            P("section", ("groups", "col"), "row"),
            P("section", ("groups", "row"), "col"),
            P(("groups", "col"), "row"),
            P("section", "row", "col"),
            P("section", "row"),
        ),
        out_specs=(P(("groups", "section"), "row", "col"), P("section", ("groups", "col"), "row")),
        check_vma=False,
    )
```
